128 devices in a mesh: seq: 8 (over y, core), exp: 16 (over z, x).
Axes of the slice: x: 4, y: 4, z: 4, core: 2. Of those that a mesh axis runs over, the one named last changes fastest.
Arguments:
- frames: bfloat16 [16, 1024, 1024], P('exp', 'seq'), may hold values from -6 to 6
- conv_kernel: float32 [31, 1024], replicated, may hold values from -1 to 1
- routes: int32 [16, 1024, 2], P('exp', 'seq'), may hold values from 0 to 63, all different within a row; in each aligned block of 128 rows (0 to 127, 128 to 255, ..., all dimensions but the last counted through in order) at most 8 rows name the same one
- gates: float32 [16, 1024, 2], P('exp', 'seq'), may hold values from 0.25 to 1
- w_in: bfloat16 [64, 1024, 2048], P('exp', None, 'seq'), may hold values from -0.1875 to 0.1875
- w_out: bfloat16 [64, 2048, 1024], P('exp', 'seq'), may hold values from -0.125 to 0.125
- cotangent: bfloat16 [16, 1024, 1024], P('exp', 'seq'), may hold values from -1.5 to 1.5
Outputs:
- mixed: bfloat16 [16, 1024, 1024], P('exp', 'seq')
- frames_grad: bfloat16 [16, 1024, 1024], P('exp', 'seq')
- w_in_grad: float32 [64, 1024, 2048], P('exp', None, 'seq')
- w_out_grad: float32 [64, 2048, 1024], P('exp', 'seq')
The draws below stay inside these ranges and needn't reach their ends.
Inputs may be any that keep to these rules, and one draw needn't show every extreme that they name: `routes`: each frame names two different experts. Within each aligned block of 128 frames of a recording no expert is named more than 8 times, and in every draw some expert is named exactly 8 times within some block.
All inputs are finite; a program needn't handle non-finite values.
Results may differ from the reference program's by a relative error of at most 0.012.
Values may be sent and summed in bfloat16 or wider, within the bound.
No kernel may reach another device: no remote copies, remote signals or barrier semaphores. Data moves between devices by JAX's collectives and lax.ppermute only.
A program may use at most 192 MiB of HBM per device.

```python
import math
import jax
import jax.numpy as jnp
import numpy as np
from jax import lax

D = 1024
HID = 2048
KERNEL = 31
T_DEV = 128
CAP = 8
EXPERTS = 64
LEN = 1024
HID_DEV = 256
N_SEQ = 8
N_EXP = 16


def steps_of(own_key, shape, pieces, low, high):
    def one(dim, blocks):
        draws = jax.random.uniform(jax.random.fold_in(jax.random.fold_in(own_key, 6), dim), (blocks,), jnp.float32, low / len(pieces), high / len(pieces))
        return jnp.repeat(jnp.exp(draws), shape[dim] // blocks).reshape((-1,) + (1,) * (len(shape) - dim - 1))

    gain = one(*pieces[0])
    for cut in pieces[1:]:
        gain = gain * one(*cut)
    return gain


def deal_out(stream_key, own, number, rows, amount, top, bound, skew):
    order = jax.random.permutation(stream_key, amount)
    heavy_load, common = shares(amount, rows * top, bound, skew, True), shares(amount, rows * top, bound, skew, False)
    places = jnp.arange(amount)

    def named(lengths, offset_by):
        used = int((lengths > 0).sum())
        fixed = max(1, used // 4)
        passed = fixed + (places - fixed + offset_by * (used - fixed)) % max(1, amount - fixed)
        return jnp.zeros((amount,), jnp.int32).at[order[jnp.where(places < fixed, places, passed)]].set(jnp.asarray(lengths, jnp.int32))

    lengths = jnp.where(number % 4 == 0, named(heavy_load, number // 4), named(common, number - number // 4 - 1))
    mixed = jax.random.permutation(jax.random.fold_in(own, 3), amount)
    donor, taker = mixed[0:amount // 2 * 2:2], mixed[1:amount // 2 * 2:2]
    room = jnp.minimum(lengths[donor] - 1, bound - lengths[taker]) // 2
    room = jnp.where((donor == order[0]) | (taker == order[0]) | (lengths[taker] == 0), 0, jnp.maximum(room, 0))
    passed = jax.random.randint(jax.random.fold_in(own, 4), (amount // 2,), 0, 1 << 20) % (room + 1)
    lengths = lengths.at[donor].add(-passed).at[taker].add(passed)
    members = jnp.searchsorted(jnp.cumsum(lengths), jnp.arange(rows * top), side="right").astype(jnp.int32)
    grid = members.reshape(top, rows).T
    grid = grid[jax.random.permutation(jax.random.fold_in(own, 1), rows)]
    offset_by = jax.random.randint(jax.random.fold_in(own, 2), (rows, 1), 0, top)
    return jnp.take_along_axis(grid, (jnp.arange(top)[None, :] + offset_by) % top, axis=1)


def shares(count, total, reach, skew, full):
    loads = [(1 << 20) // math.isqrt(rank ** skew) + 1 for rank in range(1, count + 1)]
    largest = reach if full else min(reach, max(-(-total // count), total * loads[0] // sum(loads)))
    least = 1 if total - largest >= count - 1 else 0
    counts, spare = [largest] + [least] * (count - 1), total - largest - least * (count - 1)
    while spare > 0:
        candidates = [i for i in range(1, count) if counts[i] < largest] or [i for i in range(1, count) if counts[i] < reach]
        whole, budget = sum([loads[i] for i in candidates]), spare
        for i in candidates:
            addition = min(reach - counts[i], max(1, budget * loads[i] // whole), spare)
            counts[i] = counts[i] + addition
            spare = spare - addition
    return np.array(counts)


def noise(own_key, dims, spread, bound, cuts=(), held_as=jnp.bfloat16):
    array = jax.random.normal(own_key, dims, jnp.float32) * spread
    if len(cuts) > 0:
        array = steps_of(own_key, dims, cuts, -0.22, 0.18) * array
    return jnp.clip(array, min=-bound, max=bound).astype(held_as)


def setup_inputs(seed: int = 0) -> dict:
    arg_keys = jax.random.split(jax.random.key(seed), 8)
    frames = noise(arg_keys[0], (N_EXP, LEN, D), 1.0, 6.0, ((0, 16), (1, 8)))
    conv_kernel = noise(arg_keys[1], (KERNEL, D), KERNEL ** -0.5, 1.0, (), jnp.float32)
    routes_keys = jax.random.split(jax.random.fold_in(arg_keys[2], 1), N_EXP * LEN // T_DEV)
    routes_turns = jax.random.permutation(jax.random.fold_in(arg_keys[2], 3), N_EXP * LEN // T_DEV)
    routes = jax.vmap(lambda own, number: deal_out(jax.random.fold_in(arg_keys[2], 2), own, number, T_DEV, EXPERTS, 2, CAP, 1))(routes_keys, routes_turns).reshape((N_EXP, LEN, 2))
    gates = jnp.clip(0.25 + 0.75 * jax.random.uniform(arg_keys[3], (N_EXP, LEN, 2), jnp.float32) ** steps_of(arg_keys[3], (N_EXP, LEN, 2), ((0, 16), (1, 8)), -0.2, 0.2), 0.25, 1.0)
    w_in = noise(arg_keys[4], (EXPERTS, D, HID), D ** -0.5, 0.1875, ((0, 16), (2, 8)))
    w_out = noise(arg_keys[5], (EXPERTS, HID, D), HID ** -0.5, 0.125, ((0, 16), (1, 8)))
    cotangent = noise(arg_keys[6], (N_EXP, LEN, D), 0.25, 1.5, ((0, 16), (1, 8)))
    return dict(frames=frames, conv_kernel=conv_kernel, routes=routes, gates=gates, w_in=w_in, w_out=w_out, cotangent=cotangent)


def silu_slope(values):
    logistic = jax.nn.sigmoid(values)
    return logistic * (1.0 + values * (1.0 - logistic))


def depthwise(values, kernel, reverse):
    margin = (KERNEL - 1) // 2
    padded = jnp.pad(values, ((0, 0), (margin, margin), (0, 0)))
    length = values.shape[1]
    summed = jnp.zeros_like(values)
    for tap_index in range(KERNEL):
        offset = 2 * margin - tap_index if reverse else tap_index
        summed = summed + kernel[tap_index] * padded[:, offset:offset + length, :]
    return summed


def block_sum(left, right):
    row_total = left.shape[0]
    parts = jnp.einsum("rnh,nhd->nrd", left.reshape(row_total, N_SEQ, HID_DEV).astype(jnp.float32),
                       right.reshape(N_SEQ, HID_DEV, -1).astype(jnp.float32))
    rounded = lax.optimization_barrier(parts.astype(jnp.bfloat16))
    return jnp.sum(rounded.astype(jnp.float32), axis=0).astype(jnp.bfloat16)


def expert_pass(pack):
    up_rows, down_rows, weight_in, weight_out = pack
    pre_act = jnp.dot(up_rows, weight_in, preferred_element_type=jnp.float32)
    activation = jax.nn.silu(pre_act).astype(jnp.bfloat16)
    expert_out = block_sum(activation, weight_out)
    act_grad = jnp.dot(down_rows, weight_out.T, preferred_element_type=jnp.float32)
    pre_grad = (act_grad * silu_slope(pre_act)).astype(jnp.bfloat16)
    input_grad = block_sum(pre_grad, weight_in.T)
    grad_out = jnp.dot(activation.T, down_rows, preferred_element_type=jnp.float32)
    grad_in = jnp.dot(up_rows.T, pre_grad, preferred_element_type=jnp.float32)
    return expert_out, input_grad, grad_in, grad_out


def reference(frames, conv_kernel, routes, gates, w_in, w_out, cotangent):
    mixing = depthwise(frames.astype(jnp.float32), conv_kernel, False)
    hidden = (frames.astype(jnp.float32) + jax.nn.silu(mixing)).astype(jnp.bfloat16)
    blocks = N_EXP * N_SEQ
    expert_ids = routes.reshape(blocks, 2 * T_DEV).astype(jnp.int32)
    onehot = (expert_ids[:, :, None] == jnp.arange(EXPERTS, dtype=jnp.int32)[None, None, :]).astype(jnp.int32)
    slot_rank = jnp.sum((jnp.cumsum(onehot, axis=1) - onehot) * onehot, axis=2).astype(jnp.int32)
    block_index = jnp.broadcast_to(jnp.arange(blocks, dtype=jnp.int32)[:, None], expert_ids.shape)
    up_rows = jnp.repeat(hidden.reshape(blocks, T_DEV, D), 2, axis=1)
    gate_col = gates.reshape(blocks, 2 * T_DEV, 1)
    down_rows = (gate_col * jnp.repeat(cotangent.reshape(blocks, T_DEV, D).astype(jnp.float32), 2, axis=1)).astype(jnp.bfloat16)
    blank_slots = jnp.zeros((EXPERTS, blocks, CAP, D), jnp.bfloat16)
    routed_up = blank_slots.at[expert_ids, block_index, slot_rank].set(up_rows).reshape(EXPERTS, blocks * CAP, D)
    routed_down = blank_slots.at[expert_ids, block_index, slot_rank].set(down_rows).reshape(EXPERTS, blocks * CAP, D)
    expert_outs, expert_grads, w_in_grad, w_out_grad = lax.map(expert_pass, (routed_up, routed_down, w_in, w_out))

    def collect(stacked):
        picked = stacked.reshape(EXPERTS, blocks, CAP, D)[expert_ids, block_index, slot_rank]
        return picked.reshape(N_EXP, LEN, 2, D).astype(jnp.float32)

    mixed = (hidden.astype(jnp.float32) + jnp.sum(gates[..., None] * collect(expert_outs), axis=2)).astype(jnp.bfloat16)
    hidden_grad = cotangent.astype(jnp.float32) + jnp.sum(collect(expert_grads), axis=2)
    conv_back = (hidden_grad * silu_slope(mixing)).astype(jnp.bfloat16)
    frames_grad = (hidden_grad + depthwise(conv_back.astype(jnp.float32), conv_kernel, True)).astype(jnp.bfloat16)
    return (mixed, frames_grad, w_in_grad, w_out_grad)
```

```python
import jax
import jax.numpy as jnp
from jax import lax
from jax.experimental import pallas as pl
from jax.experimental.pallas import tpu as pltpu
from jax.sharding import Mesh, PartitionSpec as P

KERNEL = 31
MARGIN = (KERNEL - 1) // 2
CAP = 8
EDGE = 16
BF16 = jnp.bfloat16
F32 = jnp.float32


def shape_of(dims, dtype):
    return jax.ShapeDtypeStruct(dims, dtype)


def params(mib):
    return pltpu.CompilerParams(vmem_limit_bytes=mib << 20)


def cost(flops, nbytes):
    return pl.CostEstimate(flops=flops, bytes_accessed=nbytes, transcendentals=0)


def silu_slope(values):
    logistic = jax.nn.sigmoid(values)
    return logistic * (1.0 + values * (1.0 - logistic))


def dot(left, right, dims):
    return lax.dot_general(left, right, ((dims[:1], dims[1:]), ((), ())), preferred_element_type=F32)


def slot_masks(routes_ref, experts, n_y):
    length = routes_ref.shape[0]
    n_exp = experts // n_y
    slots = experts * CAP
    routes = routes_ref[...]
    lane = lax.broadcasted_iota(jnp.int32, (length, experts), 1)
    before = (
        lax.broadcasted_iota(jnp.int32, (length, length), 1)
        < lax.broadcasted_iota(jnp.int32, (length, length), 0)
    ).astype(F32).astype(BF16)
    place = lax.broadcasted_iota(jnp.int32, (length, slots), 1)
    base = jnp.zeros((1, experts), F32)
    masks = []
    for choice in range(2):
        expert = routes[:, choice : choice + 1]
        named = (lane == expert).astype(F32)
        earlier = dot(before, named.astype(BF16), (1, 0)) + base
        rank = jnp.sum(named * earlier, axis=1, keepdims=True).astype(jnp.int32)
        base = base + jnp.sum(named, axis=0, keepdims=True)
        start = (expert % n_y) * n_exp + expert // n_y
        masks.append((place == start * CAP + rank).astype(F32).astype(BF16))
    return masks


def down_slots(routes, gates, cotangent, experts, n_y):
    length, width = cotangent.shape

    def body(routes_ref, gates_ref, cot_ref, out_ref):
        masks = slot_masks(routes_ref, experts, n_y)
        cot = cot_ref[...].astype(F32)
        gate = gates_ref[...]
        total = None
        for choice in range(2):
            rows = (gate[:, choice : choice + 1] * cot).astype(BF16)
            part = dot(masks[choice], rows, (0, 0))
            total = part if total is None else total + part
        out_ref[...] = total.astype(BF16)

    return pl.pallas_call(
        body,
        out_shape=shape_of((experts * CAP, width), BF16),
        compiler_params=params(32),
        cost_estimate=cost(1 << 28, 2 << 20),
        name="down_slots",
    )(routes, gates, cotangent)


def tap_sum(pad_ref, kernel_ref, columns, length, reverse):
    padded = pad_ref[:, columns]
    taps = kernel_ref[:, columns]
    total = jnp.zeros((length, padded.shape[1]), F32)
    for residue in range(8):
        offsets = [
            tap for tap in range(KERNEL) if (EDGE - MARGIN + tap) % 8 == residue
        ]
        shifted = padded[residue : residue + length + 24, :]
        for tap in offsets:
            start = EDGE - MARGIN + tap - residue
            weight = KERNEL - 1 - tap if reverse else tap
            total = total + taps[weight : weight + 1, :] * shifted[start : start + length, :]
    return total


COLUMNS = 128


def conv_up(low, frames, high, kernel, routes, experts, n_y):
    length, width = frames.shape

    def body(low_ref, frames_ref, high_ref, kernel_ref, routes_ref, mix_ref, hid_ref, out_ref, pad):
        pad[:EDGE] = low_ref[...].astype(F32)
        pad[EDGE : EDGE + length] = frames_ref[...].astype(F32)
        pad[EDGE + length :] = high_ref[...].astype(F32)

        def step(index, carry):
            columns = pl.ds(pl.multiple_of(index * COLUMNS, COLUMNS), COLUMNS)
            mixing = tap_sum(pad, kernel_ref, columns, length, False)
            mix_ref[:, columns] = mixing
            own = pad[EDGE : EDGE + length, columns]
            hid_ref[:, columns] = (own + mixing * jax.nn.sigmoid(mixing)).astype(BF16)
            return carry

        lax.fori_loop(0, width // COLUMNS, step, 0)
        first, second = slot_masks(routes_ref, experts, n_y)
        out_ref[...] = dot(first + second, hid_ref[...], (0, 0)).astype(BF16)

    return pl.pallas_call(
        body,
        out_shape=(
            shape_of((length, width), F32),
            shape_of((length, width), BF16),
            shape_of((experts * CAP, width), BF16),
        ),
        scratch_shapes=[pltpu.VMEM((length + 2 * EDGE, width), F32)],
        compiler_params=params(32),
        cost_estimate=cost(1 << 28, 3 << 20),
        name="conv_up",
    )(low, frames, high, kernel, routes)


TILE = 256


def block_step(up, down, w_in, w_out, grad_type):
    rows, width = up[0].shape
    hidden = w_in.shape[1]

    def body(ua, ub, da, db, wi, wo, act_ref, pre_ref, gi_ref, go_ref):
        for half, (u_ref, d_ref) in enumerate(((ua, da), (ub, db))):
            for start in range(0, rows, TILE):
                part = slice(start, start + TILE)
                held = slice(half * rows + start, half * rows + start + TILE)
                pre = dot(u_ref[part, :], wi[...], (1, 0))
                logistic = jax.nn.sigmoid(pre)
                act_ref[held, :] = (pre * logistic).astype(BF16)
                back = dot(d_ref[part, :], wo[...], (1, 1))
                slope = logistic * (1.0 + pre * (1.0 - logistic))
                pre_ref[held, :] = (back * slope).astype(BF16)
        for start in range(0, width, TILE):
            part = slice(start, start + TILE)
            out = dot(act_ref[:rows, :], da[:, part], (0, 0))
            out = out + dot(act_ref[rows:, :], db[:, part], (0, 0))
            go_ref[:, part] = out.astype(grad_type)
            out = dot(ua[:, part], pre_ref[:rows, :], (0, 0))
            out = out + dot(ub[:, part], pre_ref[rows:, :], (0, 0))
            gi_ref[part, :] = out.astype(grad_type)

    return pl.pallas_call(
        body,
        out_shape=(
            shape_of((2 * rows, hidden), BF16),
            shape_of((2 * rows, hidden), BF16),
            shape_of((width, hidden), grad_type),
            shape_of((hidden, width), grad_type),
        ),
        compiler_params=params(48),
        cost_estimate=cost(16 * rows * width * hidden, 8 << 20),
        name="block_step",
    )(up[0], up[1], down[0], down[1], w_in, w_out)


def back_to_width(parts, weights, contract, rows):
    width = weights[0].shape[1 - contract]

    def body(*refs):
        part_refs, weight_refs = refs[:4], refs[4:8]
        own_ref, other_ref = refs[8:]
        for half, out_ref in enumerate((own_ref, other_ref)):
            for start in range(0, rows, TILE):
                held = slice(half * rows + start, half * rows + start + TILE)
                total = None
                for part_ref, weight_ref in zip(part_refs, weight_refs):
                    part = dot(part_ref[held, :], weight_ref[...], (1, contract))
                    total = part if total is None else total + part
                out_ref[start : start + TILE, :] = total.astype(BF16)

    return pl.pallas_call(
        body,
        out_shape=(shape_of((rows, width), BF16), shape_of((rows, width), BF16)),
        compiler_params=params(48),
        cost_estimate=cost(16 * rows * width * 256, 8 << 20),
        name="back_to_width",
    )(*parts, *weights)


def mix_out(routes, gates, hidden, expert_out, experts, n_y):
    def body(routes_ref, gates_ref, hid_ref, out_ref, mixed_ref):
        masks = slot_masks(routes_ref, experts, n_y)
        gate = gates_ref[...]
        total = hid_ref[...].astype(F32)
        for choice in range(2):
            total = total + gate[:, choice : choice + 1] * dot(masks[choice], out_ref[...], (1, 0))
        mixed_ref[...] = total.astype(BF16)

    return pl.pallas_call(
        body,
        out_shape=shape_of(hidden.shape, BF16),
        compiler_params=params(32),
        cost_estimate=cost(1 << 28, 2 << 20),
        name="mix_out",
    )(routes, gates, hidden, expert_out)


def grad_rows(routes, cotangent, mixing, input_grad, experts, n_y):
    def body(routes_ref, cot_ref, mix_ref, grad_ref, hidden_ref, back_ref):
        first, second = slot_masks(routes_ref, experts, n_y)
        grad = cot_ref[...].astype(F32) + dot(first + second, grad_ref[...], (1, 0))
        hidden_ref[...] = grad
        back_ref[...] = (grad * silu_slope(mix_ref[...])).astype(BF16)

    return pl.pallas_call(
        body,
        out_shape=(shape_of(cotangent.shape, F32), shape_of(cotangent.shape, BF16)),
        compiler_params=params(32),
        cost_estimate=cost(1 << 28, 3 << 20),
        name="grad_rows",
    )(routes, cotangent, mixing, input_grad)


def conv_down(low, back, high, kernel, hidden_grad):
    length, width = back.shape

    def body(low_ref, back_ref, high_ref, kernel_ref, grad_ref, out_ref, pad):
        pad[:EDGE] = low_ref[...].astype(F32)
        pad[EDGE : EDGE + length] = back_ref[...].astype(F32)
        pad[EDGE + length :] = high_ref[...].astype(F32)

        def step(index, carry):
            columns = pl.ds(pl.multiple_of(index * COLUMNS, COLUMNS), COLUMNS)
            spread = tap_sum(pad, kernel_ref, columns, length, True)
            out_ref[:, columns] = (grad_ref[:, columns] + spread).astype(BF16)
            return carry

        lax.fori_loop(0, width // COLUMNS, step, 0)

    return pl.pallas_call(
        body,
        out_shape=shape_of((length, width), BF16),
        scratch_shapes=[pltpu.VMEM((length + 2 * EDGE, width), F32)],
        compiler_params=params(32),
        cost_estimate=cost(1 << 27, 2 << 20),
        name="conv_down",
    )(low, back, high, kernel, hidden_grad)


def place_grads(spots, parts):
    rows, columns = parts[0].shape
    count = len(parts)

    def body(spots_ref, *refs):
        part_refs, out_ref = refs[:count], refs[count]
        for index in range(count):

            @pl.when(pl.program_id(0) == index)
            def _():
                out_ref[0] = part_refs[index][...].astype(F32)

    return pl.pallas_call(
        body,
        grid_spec=pltpu.PrefetchScalarGridSpec(
            num_scalar_prefetch=1,
            grid=(count,),
            in_specs=[
                pl.BlockSpec((rows, columns), lambda i, spots: (0, 0)) for _ in range(count)
            ],
            out_specs=pl.BlockSpec((1, rows, columns), lambda i, spots: (spots[i], 0, 0)),
        ),
        out_shape=shape_of((count, rows, columns), F32),
        compiler_params=params(32),
        cost_estimate=cost(1 << 20, 7 << 20),
        name="place_grads",
    )(spots, *parts)


def edges(block):
    count = lax.axis_size("y") * lax.axis_size("core")
    forward = [(i, i + 1) for i in range(count - 1)]
    backward = [(target, source) for source, target in forward]
    low = lax.ppermute(block[-EDGE:], ("y", "core"), forward)
    high = lax.ppermute(block[:EDGE], ("y", "core"), backward)
    return low, high


def turn(block, steps):
    count = lax.axis_size("y")
    return lax.ppermute(block, "y", [(i, (i + steps) % count) for i in range(count)])


def swap(block):
    return lax.ppermute(block, "core", [(0, 1), (1, 0)])


def exchange(rows, groups):
    grouped = rows.reshape(groups, CAP, rows.shape[1])
    moved = lax.all_to_all(grouped, ("y", "exp"), split_axis=0, concat_axis=0, tiled=True)
    return moved.reshape(rows.shape)


def per_device(frames, conv_kernel, routes, gates, w_in, w_out, cotangent):
    n_y = lax.axis_size("y")
    n_exp = lax.axis_size("exp")
    groups = n_y * n_exp
    experts = w_in.shape[0] * n_exp
    y = lax.axis_index("y")
    frames, routes, gates, cotangent = frames[0], routes[0], gates[0], cotangent[0]
    slots = experts * CAP

    low, high = edges(frames)

    def gathered(weights):
        def block(steps):
            return lax.dynamic_index_in_dim(weights, (y + steps) % n_y, 0, keepdims=False)

        return [block(0)] + [turn(block(steps), steps) for steps in range(1, n_y)]

    w_ins = gathered(w_in)
    w_outs = gathered(w_out)

    send_down = down_slots(routes, gates, cotangent, experts, n_y)
    down = exchange(send_down, groups)
    mixing, hidden, send_up = conv_up(low, frames, high, conv_kernel, routes, experts, n_y)
    up = exchange(send_up, groups)
    downs = (down, swap(down))
    ups = (up, swap(up))

    acts, pres, grads_in, grads_out = [], [], [], []
    for steps in range(n_y):
        kept = F32 if steps == 0 else BF16
        act, pre, grad_in, grad_out = block_step(ups, downs, w_ins[steps], w_outs[steps], kept)
        acts.append(act)
        pres.append(pre)
        if steps:
            grad_in, grad_out = turn(grad_in, -steps), turn(grad_out, -steps)
        grads_in.append(grad_in)
        grads_out.append(grad_out)

    own, other = back_to_width(pres, w_ins, 1, slots)
    input_grad = exchange((own.astype(F32) + swap(other).astype(F32)).astype(BF16), groups)
    own, other = back_to_width(acts, w_outs, 0, slots)
    expert_out = exchange((own.astype(F32) + swap(other).astype(F32)).astype(BF16), groups)

    hidden_grad, back = grad_rows(routes, cotangent, mixing, input_grad, experts, n_y)
    low, high = edges(back)
    frames_grad = conv_down(low, back, high, conv_kernel, hidden_grad)
    mixed = mix_out(routes, gates, hidden, expert_out, experts, n_y)

    spots = jnp.stack([(y + steps) % n_y for steps in range(n_y)]).astype(jnp.int32)
    w_in_grad = place_grads(spots, grads_in)
    w_out_grad = place_grads(spots, grads_out)
    return (mixed[None], frames_grad[None], w_in_grad, w_out_grad)


def solution(mesh):
    cores = 2
    n_seq, n_exp = mesh.devices.shape
    split = Mesh(mesh.devices.reshape(n_seq // cores, cores, n_exp), ("y", "core", "exp"))
    seq = ("y", "core")
    in_specs = (
        P("exp", seq, None),
        P(),
        P("exp", seq, None),
        P("exp", seq, None),
        P("exp", None, seq),
        P("exp", seq, None),
        P("exp", seq, None),
    )
    out_specs = (
        P("exp", seq, None),
        P("exp", seq, None),
        P("exp", None, seq),
        P("exp", seq, None),
    )
    return jax.shard_map(
        per_device, mesh=split, in_specs=in_specs, out_specs=out_specs, check_vma=False
    )
```

```python
import jax
import jax.numpy as jnp
from jax import lax
from jax.experimental import pallas as pl
from jax.experimental.pallas import tpu as pltpu
from jax.sharding import Mesh, PartitionSpec as P

KERNEL = 31
MARGIN = (KERNEL - 1) // 2
CAP = 8
EDGE = 16
BF16 = jnp.bfloat16
F32 = jnp.float32


def shape_of(dims, dtype):
    return jax.ShapeDtypeStruct(dims, dtype)


def params(mib):
    return pltpu.CompilerParams(vmem_limit_bytes=mib << 20)


COST = pl.CostEstimate(flops=1, bytes_accessed=1, transcendentals=0)


def silu_slope(values):
    logistic = jax.nn.sigmoid(values)
    return logistic * (1.0 + values * (1.0 - logistic))


def dot(left, right, dims):
    return lax.dot_general(left, right, ((dims[:1], dims[1:]), ((), ())), preferred_element_type=F32)


def slot_masks(routes_ref, experts, n_y):
    length = routes_ref.shape[0]
    n_exp = experts // n_y
    slots = experts * CAP
    routes = routes_ref[...]
    lane = lax.broadcasted_iota(jnp.int32, (length, experts), 1)
    before = (
        lax.broadcasted_iota(jnp.int32, (length, length), 1)
        < lax.broadcasted_iota(jnp.int32, (length, length), 0)
    ).astype(F32).astype(BF16)
    place = lax.broadcasted_iota(jnp.int32, (length, slots), 1)
    base = jnp.zeros((1, experts), F32)
    masks = []
    for choice in range(2):
        expert = routes[:, choice : choice + 1]
        named = (lane == expert).astype(F32)
        earlier = dot(before, named.astype(BF16), (1, 0)) + base
        rank = jnp.sum(named * earlier, axis=1, keepdims=True).astype(jnp.int32)
        base = base + jnp.sum(named, axis=0, keepdims=True)
        start = (expert % n_y) * n_exp + expert // n_y
        masks.append((place == start * CAP + rank).astype(F32).astype(BF16))
    return masks


def down_slots(routes, gates, cotangent, experts, n_y):
    length, width = cotangent.shape

    def body(routes_ref, gates_ref, cot_ref, out_ref):
        masks = slot_masks(routes_ref, experts, n_y)
        cot = cot_ref[...].astype(F32)
        gate = gates_ref[...]
        total = None
        for choice in range(2):
            rows = (gate[:, choice : choice + 1] * cot).astype(BF16)
            part = dot(masks[choice], rows, (0, 0))
            total = part if total is None else total + part
        out_ref[...] = total.astype(BF16)

    return pl.pallas_call(
        body,
        grid=(1,),
        in_specs=[
            pl.BlockSpec(routes.shape, lambda i: (0, 0)),
            pl.BlockSpec(gates.shape, lambda i: (0, 0)),
            pl.BlockSpec(cotangent.shape, lambda i: (0, 0)),
        ],
        out_specs=pl.BlockSpec((experts * CAP, width), lambda i: (0, 1)),
        out_shape=shape_of((experts * CAP, 2 * width), BF16),
        compiler_params=params(32),
        cost_estimate=COST,
        name="down_slots",
    )(routes, gates, cotangent)


def tap_sum(pad_ref, kernel_ref, columns, length, reverse):
    padded = pad_ref[:, columns]
    taps = kernel_ref[:, columns]
    total = jnp.zeros((length, padded.shape[1]), F32)
    for residue in range(8):
        offsets = [
            tap for tap in range(KERNEL) if (EDGE - MARGIN + tap) % 8 == residue
        ]
        shifted = padded[residue : residue + length + 24, :]
        for tap in offsets:
            start = EDGE - MARGIN + tap - residue
            weight = KERNEL - 1 - tap if reverse else tap
            total = total + taps[weight : weight + 1, :] * shifted[start : start + length, :]
    return total


COLUMNS = 128


def conv_up(low, frames, high, kernel, routes, send, experts, n_y):
    length, width = frames.shape
    slots = experts * CAP

    def body(low_ref, frames_ref, high_ref, kernel_ref, routes_ref, _, mix_ref, hid_ref, out_ref, pad):
        pad[:EDGE] = low_ref[...].astype(F32)
        pad[EDGE : EDGE + length] = frames_ref[...].astype(F32)
        pad[EDGE + length :] = high_ref[...].astype(F32)

        def step(index, carry):
            columns = pl.ds(pl.multiple_of(index * COLUMNS, COLUMNS), COLUMNS)
            mixing = tap_sum(pad, kernel_ref, columns, length, False)
            mix_ref[:, columns] = mixing
            own = pad[EDGE : EDGE + length, columns]
            hid_ref[:, columns] = (own + mixing * jax.nn.sigmoid(mixing)).astype(BF16)
            return carry

        lax.fori_loop(0, width // COLUMNS, step, 0)
        first, second = slot_masks(routes_ref, experts, n_y)
        out_ref[...] = dot(first + second, hid_ref[...], (0, 0)).astype(BF16)

    operands = (low, frames, high, kernel, routes)
    return pl.pallas_call(
        body,
        grid=(1,),
        in_specs=[pl.BlockSpec(o.shape, lambda i: (0, 0)) for o in operands]
        + [pl.BlockSpec(memory_space=pl.ANY)],
        out_specs=(
            pl.BlockSpec((length, width), lambda i: (0, 0)),
            pl.BlockSpec((length, width), lambda i: (0, 0)),
            pl.BlockSpec((slots, width), lambda i: (0, 0)),
        ),
        out_shape=(
            shape_of((length, width), F32),
            shape_of((length, width), BF16),
            shape_of((slots, 2 * width), BF16),
        ),
        input_output_aliases={5: 2},
        scratch_shapes=[pltpu.VMEM((length + 2 * EDGE, width), F32)],
        compiler_params=params(32),
        cost_estimate=COST,
        name="conv_up",
    )(*operands, send)


TILE = 256


def copy_all(copies):
    for copy in copies:
        copy.start()
    for copy in copies:
        copy.wait()


def pack_weights(spots, w_in, w_out):
    _, width, hidden = w_in.shape
    pieces = width // hidden
    half = width // 2

    def body(spots_ref, in_ref, out_ref, own_ref, first_up, first_down, next_up, next_down, sems):
        copies = []

        def move(source, target):
            copies.append(pltpu.make_async_copy(source, target, sems.at[len(copies)]))

        def pack(steps, low, high, ref, offset):
            spot = spots_ref[steps]
            move(
                in_ref.at[spot, pl.ds(low, high - low)],
                ref.at[pl.ds(offset, high - low), :hidden],
            )
            for start in range(low, high, hidden):
                move(
                    out_ref.at[spot, :, pl.ds(start, hidden)],
                    ref.at[pl.ds(offset + start - low, hidden), hidden:],
                )

        pack(2, 0, half, first_up, 0)
        pack(2, half, width, first_down, 0)
        pack(1, 0, width, next_up, half)
        pack(3, 0, width, next_down, half)
        pack(0, 0, width, own_ref, 0)
        copy_all(copies)

    rows = (width, half, half, width + half, width + half)
    return pl.pallas_call(
        body,
        in_specs=[pl.BlockSpec(memory_space=pltpu.SMEM)] + [pl.BlockSpec(memory_space=pl.ANY)] * 2,
        out_specs=[pl.BlockSpec(memory_space=pl.ANY)] * len(rows),
        out_shape=[shape_of((count, 2 * hidden), BF16) for count in rows],
        scratch_shapes=[pltpu.SemaphoreType.DMA((4 * (1 + pieces) + 1,))],
        compiler_params=params(16),
        cost_estimate=COST,
        name="pack_weights",
    )(spots, w_in, w_out)


def fill_first(parts, wholes):
    count = parts[0].shape[0]

    def body(*refs):
        sems = refs[-1]
        copy_all(
            [
                pltpu.make_async_copy(refs[i], refs[4 + i].at[:count], sems.at[i])
                for i in range(2)
            ]
        )

    return pl.pallas_call(
        body,
        in_specs=[pl.BlockSpec(memory_space=pl.ANY)] * 4,
        out_specs=[pl.BlockSpec(memory_space=pl.ANY)] * 2,
        out_shape=[shape_of(whole.shape, BF16) for whole in wholes],
        input_output_aliases={2: 0, 3: 1},
        scratch_shapes=[pltpu.SemaphoreType.DMA((2,))],
        compiler_params=params(16),
        cost_estimate=COST,
        name="fill_first",
    )(*parts, *wholes)


def half_specs(halves):
    rows = []
    for array, index in halves:
        block = (array.shape[1], array.shape[1])
        rows.append(pl.BlockSpec(block, lambda i, index=index: (index, 0)))
    return rows


def whole_spec(array):
    return pl.BlockSpec(array.shape, lambda i: (0, 0))


def split_in(lows, halves, hidden):
    total = None
    step = halves[0].shape[0]
    for index, ref in enumerate(halves):
        part = dot(lows[:, index * step : (index + 1) * step], ref[:, :hidden], (1, 0))
        total = part if total is None else total + part
    return total


def out_piece(halves, piece, hidden):
    step = halves[0].shape[0]
    ref = halves[piece // step]
    start = piece % step
    return ref[start : start + hidden, hidden:]


def activate(rows, refs, halves, act_ref, pre_ref):
    hidden = halves[0].shape[1] // 2
    width = refs[0].shape[1] // 2
    for half, ref in enumerate(refs):
        for start in range(0, rows, TILE):
            part = slice(start, start + TILE)
            held = slice(half * rows + start, half * rows + start + TILE)
            pre = split_in(ref[part, :width], halves, hidden)
            logistic = jax.nn.sigmoid(pre)
            act_ref[held, :] = (pre * logistic).astype(BF16)
            back = None
            for piece in range(0, width, hidden):
                term = dot(
                    ref[part, width + piece : width + piece + hidden],
                    out_piece(halves, piece, hidden),
                    (1, 1),
                )
                back = term if back is None else back + term
            slope = logistic * (1.0 + pre * (1.0 - logistic))
            pre_ref[held, :] = (back * slope).astype(BF16)


def weigh(rows, refs, act_ref, pre_ref, grad_ref):
    width, hidden = grad_ref.shape[0], grad_ref.shape[1] // 2
    first, second = refs
    for piece in range(0, width, hidden):
        part = slice(piece, piece + hidden)
        shifted = slice(width + piece, width + piece + hidden)
        out = dot(act_ref[:rows, :], first[:, shifted], (0, 0))
        out = out + dot(act_ref[rows:, :], second[:, shifted], (0, 0))
        grad_ref[part, hidden:] = out.astype(grad_ref.dtype)
        out = dot(first[:, part], pre_ref[:rows, :], (0, 0))
        out = out + dot(second[:, part], pre_ref[rows:, :], (0, 0))
        grad_ref[part, :hidden] = out.astype(grad_ref.dtype)


def block_step(own, other, halves, grad_type):
    rows, width = own.shape[0], own.shape[1] // 2
    hidden = halves[0][0].shape[1] // 2
    result = [shape_of((2 * rows, hidden), BF16), shape_of((2 * rows, hidden), BF16)]
    if grad_type is not None:
        result.append(shape_of((width, 2 * hidden), grad_type))

    def body(own_ref, other_ref, low_ref, high_ref, act_ref, pre_ref, *grads):
        activate(rows, (own_ref, other_ref), (low_ref, high_ref), act_ref, pre_ref)
        for grad_ref in grads:
            weigh(rows, (own_ref, other_ref), act_ref, pre_ref, grad_ref)

    return pl.pallas_call(
        body,
        grid=(1,),
        in_specs=[whole_spec(own), whole_spec(other)] + half_specs(halves),
        out_specs=[whole_spec(array) for array in result],
        out_shape=result,
        compiler_params=params(48),
        cost_estimate=COST,
        name="block_step",
    )(own, other, *[array for array, _ in halves])


def block_grads(own, other, act, pre, grad_type):
    rows, width = own.shape[0], own.shape[1] // 2
    hidden = act.shape[1]

    def body(own_ref, other_ref, act_ref, pre_ref, grad_ref):
        weigh(rows, (own_ref, other_ref), act_ref, pre_ref, grad_ref)

    return pl.pallas_call(
        body,
        out_shape=shape_of((width, 2 * hidden), grad_type),
        compiler_params=params(48),
        cost_estimate=COST,
        name="block_grads",
    )(own, other, act, pre)


def back_to_width(half, acts, pres, packed, arrived):
    hidden = acts[0].shape[1]
    rows = acts[0].shape[0] // 2
    count = len(acts)
    width = hidden * count
    extra = [] if arrived is None else [arrived]

    def body(*refs):
        act_refs, pre_refs = refs[:count], refs[count : 2 * count]
        w_refs = [refs[2 * count + 2 * i : 2 * count + 2 * i + 2] for i in range(count)]
        out_ref = refs[-1]
        for start in range(0, rows, TILE):
            held = slice(start, start + TILE)

            def emit(columns, total):
                if extra:
                    total = total + refs[4 * count][held, columns].astype(F32)
                out_ref[held, columns] = total.astype(BF16)

            for piece in range(0, width, hidden):
                total = None
                for part_ref, halves in zip(act_refs, w_refs):
                    part = dot(part_ref[held, :], out_piece(halves, piece, hidden), (1, 0))
                    total = part if total is None else total + part
                emit(slice(piece, piece + hidden), total)
            for side in range(2):
                total = None
                for part_ref, halves in zip(pre_refs, w_refs):
                    part = dot(part_ref[held, :], halves[side][:, :hidden], (1, 1))
                    total = part if total is None else total + part
                step = width // 2
                emit(slice(width + side * step, width + (side + 1) * step), total)

    one = pl.BlockSpec((rows, hidden), lambda i: (half, 0))
    result = shape_of((rows, 2 * width), BF16)
    listed = [pair for halves in packed for pair in halves]
    return pl.pallas_call(
        body,
        grid=(1,),
        in_specs=[one] * (2 * count) + half_specs(listed) + [whole_spec(result)] * len(extra),
        out_specs=whole_spec(result),
        out_shape=result,
        compiler_params=params(48),
        cost_estimate=COST,
        name="back_to_width",
    )(*acts, *pres, *[array for array, _ in listed], *extra)


def mix_out(routes, gates, hidden, returned, experts, n_y):
    def body(routes_ref, gates_ref, hid_ref, out_ref, mixed_ref):
        masks = slot_masks(routes_ref, experts, n_y)
        gate = gates_ref[...]
        total = hid_ref[...].astype(F32)
        for choice in range(2):
            total = total + gate[:, choice : choice + 1] * dot(masks[choice], out_ref[...], (1, 0))
        mixed_ref[...] = total.astype(BF16)

    return pl.pallas_call(
        body,
        grid=(1,),
        in_specs=[
            pl.BlockSpec(routes.shape, lambda i: (0, 0)),
            pl.BlockSpec(gates.shape, lambda i: (0, 0)),
            pl.BlockSpec(hidden.shape, lambda i: (0, 0)),
            pl.BlockSpec((returned.shape[0], hidden.shape[1]), lambda i: (0, 0)),
        ],
        out_specs=pl.BlockSpec(hidden.shape, lambda i: (0, 0)),
        out_shape=shape_of(hidden.shape, BF16),
        compiler_params=params(32),
        cost_estimate=COST,
        name="mix_out",
    )(routes, gates, hidden, returned)


def grad_rows(routes, cotangent, mixing, returned, experts, n_y):
    def body(routes_ref, cot_ref, mix_ref, grad_ref, hidden_ref, back_ref):
        first, second = slot_masks(routes_ref, experts, n_y)
        grad = cot_ref[...].astype(F32) + dot(first + second, grad_ref[...], (1, 0))
        hidden_ref[...] = grad
        back_ref[...] = (grad * silu_slope(mix_ref[...])).astype(BF16)

    return pl.pallas_call(
        body,
        grid=(1,),
        in_specs=[
            pl.BlockSpec(routes.shape, lambda i: (0, 0)),
            pl.BlockSpec(cotangent.shape, lambda i: (0, 0)),
            pl.BlockSpec(mixing.shape, lambda i: (0, 0)),
            pl.BlockSpec((returned.shape[0], mixing.shape[1]), lambda i: (0, 1)),
        ],
        out_specs=(
            pl.BlockSpec(cotangent.shape, lambda i: (0, 0)),
            pl.BlockSpec(cotangent.shape, lambda i: (0, 0)),
        ),
        out_shape=(shape_of(cotangent.shape, F32), shape_of(cotangent.shape, BF16)),
        compiler_params=params(32),
        cost_estimate=COST,
        name="grad_rows",
    )(routes, cotangent, mixing, returned)


def conv_down(low, back, high, kernel, hidden_grad):
    length, width = back.shape

    def body(low_ref, back_ref, high_ref, kernel_ref, grad_ref, out_ref, pad):
        pad[:EDGE] = low_ref[...].astype(F32)
        pad[EDGE : EDGE + length] = back_ref[...].astype(F32)
        pad[EDGE + length :] = high_ref[...].astype(F32)

        def step(index, carry):
            columns = pl.ds(pl.multiple_of(index * COLUMNS, COLUMNS), COLUMNS)
            spread = tap_sum(pad, kernel_ref, columns, length, True)
            out_ref[:, columns] = (grad_ref[:, columns] + spread).astype(BF16)
            return carry

        lax.fori_loop(0, width // COLUMNS, step, 0)

    return pl.pallas_call(
        body,
        out_shape=shape_of((length, width), BF16),
        scratch_shapes=[pltpu.VMEM((length + 2 * EDGE, width), F32)],
        compiler_params=params(32),
        cost_estimate=COST,
        name="conv_down",
    )(low, back, high, kernel, hidden_grad)


def place_grads(spot, packed, count, held):
    width, hidden = packed.shape[0], packed.shape[1] // 2

    def body(spot_ref, packed_ref, *refs):
        in_ref, out_ref = refs[-2:]
        in_ref[0] = packed_ref[:, :hidden].astype(F32)
        for piece in range(0, width, hidden):
            part = slice(piece, piece + hidden)
            out_ref[0, :, part] = packed_ref[part, hidden:].astype(F32)

    return pl.pallas_call(
        body,
        grid_spec=pltpu.PrefetchScalarGridSpec(
            num_scalar_prefetch=1,
            grid=(1,),
            in_specs=[pl.BlockSpec(packed.shape, lambda i, spot: (0, 0))]
            + [pl.BlockSpec(memory_space=pl.ANY)] * len(held),
            out_specs=(
                pl.BlockSpec((1, width, hidden), lambda i, spot: (spot[0], 0, 0)),
                pl.BlockSpec((1, hidden, width), lambda i, spot: (spot[0], 0, 0)),
            ),
        ),
        out_shape=(
            shape_of((count, width, hidden), F32),
            shape_of((count, hidden, width), F32),
        ),
        input_output_aliases={2 + index: index for index in range(len(held))},
        compiler_params=params(32),
        cost_estimate=COST,
        name="place_grads",
    )(spot, packed, *held)


def edges(block):
    count = lax.axis_size("y") * lax.axis_size("core")
    forward = [(i, i + 1) for i in range(count - 1)]
    backward = [(target, source) for source, target in forward]
    low = lax.ppermute(block[-EDGE:], ("y", "core"), forward)
    high = lax.ppermute(block[:EDGE], ("y", "core"), backward)
    return low, high


def turn(block, steps):
    count = lax.axis_size("y")
    return lax.ppermute(block, "y", [(i, (i + steps) % count) for i in range(count)])


def swap(block):
    return lax.ppermute(block, "core", [(0, 1), (1, 0)])


def together(rows):
    half = rows.shape[0] // 2
    return jnp.concatenate([swap(rows[:half]), swap(rows[half:])])


def exchange(rows, groups):
    grouped = rows.reshape(groups, CAP, rows.shape[1])
    moved = lax.all_to_all(grouped, ("y", "exp"), split_axis=0, concat_axis=0, tiled=True)
    return moved.reshape(rows.shape)


def per_device(frames, conv_kernel, routes, gates, w_in, w_out, cotangent):
    n_y = lax.axis_size("y")
    n_exp = lax.axis_size("exp")
    groups = n_y * n_exp
    experts = w_in.shape[0] * n_exp
    y = lax.axis_index("y")
    frames, routes, gates, cotangent = frames[0], routes[0], gates[0], cotangent[0]
    spots = (y + jnp.arange(n_y, dtype=jnp.int32)) % n_y

    low, high = edges(frames)
    own_block, first_up, first_down, next_up, next_down = pack_weights(spots, w_in, w_out)
    first_up, first_down = turn(first_up, 1), turn(first_down, -1)

    send = down_slots(routes, gates, cotangent, experts, n_y)
    mixing, hidden, send = conv_up(low, frames, high, conv_kernel, routes, send, experts, n_y)
    send, first_up, first_down = lax.optimization_barrier((send, first_up, first_down))
    own = exchange(send, groups)
    next_up, next_down = fill_first((first_up, first_down), (next_up, next_down))
    next_up, next_down = turn(next_up, 1), turn(next_down, -1)
    other = together(own)

    order = [0, 1, 3, 2]
    acts, pres, grads = {}, {}, {}
    packed = {0: [(own_block, 0), (own_block, 1)]}
    acts[0], pres[0], grads[0] = block_step(own, other, packed[0], F32)
    acts[0], next_up, next_down = lax.optimization_barrier((acts[0], next_up, next_down))
    packed[1] = [(next_up, 1), (next_up, 2)]
    packed[3] = [(next_down, 1), (next_down, 2)]
    packed[2] = [(next_up, 0), (next_down, 0)]
    for steps in (1, 3):
        acts[steps], pres[steps], grads[steps] = block_step(own, other, packed[steps], BF16)
        grads[steps] = turn(grads[steps], -steps)
    acts[2], pres[2] = block_step(own, other, packed[2], None)
    listed = [[held[steps] for steps in order] for held in (acts, pres, packed)]
    arrived = swap(back_to_width(1, *listed, None))
    grads[2] = block_grads(own, other, acts[2], pres[2], BF16)
    arrived, grads[2] = lax.optimization_barrier((arrived, grads[2]))
    grads[2] = turn(grads[2], -2)
    result = back_to_width(0, *listed, arrived)
    result, grads[1], grads[3] = lax.optimization_barrier((result, grads[1], grads[3]))
    returned = exchange(result, groups)

    hidden_grad, back = grad_rows(routes, cotangent, mixing, returned, experts, n_y)
    low, high = edges(back)
    frames_grad = conv_down(low, back, high, conv_kernel, hidden_grad)
    mixed = mix_out(routes, gates, hidden, returned, experts, n_y)

    held = ()
    for steps in order:
        held = place_grads(spots[steps : steps + 1], grads[steps], n_y, held)
    w_in_grad, w_out_grad = held
    return (mixed[None], frames_grad[None], w_in_grad, w_out_grad)


def solution(mesh):
    cores = 2
    n_seq, n_exp = mesh.devices.shape
    split = Mesh(mesh.devices.reshape(n_seq // cores, cores, n_exp), ("y", "core", "exp"))
    seq = ("y", "core")
    in_specs = (
        P("exp", seq, None),
        P(),
        P("exp", seq, None),
        P("exp", seq, None),
        P("exp", None, seq),
        P("exp", seq, None),
        P("exp", seq, None),
    )
    out_specs = (
        P("exp", seq, None),
        P("exp", seq, None),
        P("exp", None, seq),
        P("exp", seq, None),
    )
    return jax.shard_map(
        per_device, mesh=split, in_specs=in_specs, out_specs=out_specs, check_vma=False
    )
```

```python
import jax
import jax.numpy as jnp
from jax import lax
from jax.experimental import pallas as pl
from jax.experimental.pallas import tpu as pltpu
from jax.sharding import Mesh, PartitionSpec as P

KERNEL = 31
MARGIN = (KERNEL - 1) // 2
CAP = 8
EDGE = 16
BF16 = jnp.bfloat16
F32 = jnp.float32


def shape_of(dims, dtype):
    return jax.ShapeDtypeStruct(dims, dtype)


def params(mib):
    return pltpu.CompilerParams(vmem_limit_bytes=mib << 20)


COST = pl.CostEstimate(flops=1, bytes_accessed=1, transcendentals=0)


def silu_slope(values):
    logistic = jax.nn.sigmoid(values)
    return logistic * (1.0 + values * (1.0 - logistic))


def dot(left, right, dims):
    return lax.dot_general(left, right, ((dims[:1], dims[1:]), ((), ())), preferred_element_type=F32)


def slot_masks(routes_ref, experts, n_y):
    length = routes_ref.shape[0]
    n_exp = experts // n_y
    slots = experts * CAP
    routes = routes_ref[...]
    lane = lax.broadcasted_iota(jnp.int32, (length, experts), 1)
    before = (
        lax.broadcasted_iota(jnp.int32, (length, length), 1)
        < lax.broadcasted_iota(jnp.int32, (length, length), 0)
    ).astype(F32).astype(BF16)
    place = lax.broadcasted_iota(jnp.int32, (length, slots), 1)
    base = jnp.zeros((1, experts), F32)
    masks = []
    for choice in range(2):
        expert = routes[:, choice : choice + 1]
        named = (lane == expert).astype(F32)
        earlier = dot(before, named.astype(BF16), (1, 0)) + base
        rank = jnp.sum(named * earlier, axis=1, keepdims=True).astype(jnp.int32)
        base = base + jnp.sum(named, axis=0, keepdims=True)
        start = (expert % n_y) * n_exp + expert // n_y
        masks.append((place == start * CAP + rank).astype(F32).astype(BF16))
    return masks


def down_slots(routes, gates, cotangent, experts, n_y):
    length, width = cotangent.shape

    def body(routes_ref, gates_ref, cot_ref, out_ref):
        masks = slot_masks(routes_ref, experts, n_y)
        cot = cot_ref[...].astype(F32)
        gate = gates_ref[...]
        total = None
        for choice in range(2):
            rows = (gate[:, choice : choice + 1] * cot).astype(BF16)
            part = dot(masks[choice], rows, (0, 0))
            total = part if total is None else total + part
        out_ref[...] = total.astype(BF16)

    return pl.pallas_call(
        body,
        grid=(1,),
        in_specs=[
            pl.BlockSpec(routes.shape, lambda i: (0, 0)),
            pl.BlockSpec(gates.shape, lambda i: (0, 0)),
            pl.BlockSpec(cotangent.shape, lambda i: (0, 0)),
        ],
        out_specs=pl.BlockSpec((experts * CAP, width), lambda i: (0, 1)),
        out_shape=shape_of((experts * CAP, 2 * width), BF16),
        compiler_params=params(32),
        cost_estimate=COST,
        name="down_slots",
    )(routes, gates, cotangent)


def tap_sum(pad_ref, kernel_ref, columns, length, reverse):
    padded = pad_ref[:, columns]
    taps = kernel_ref[:, columns]
    total = jnp.zeros((length, padded.shape[1]), F32)
    for residue in range(8):
        offsets = [
            tap for tap in range(KERNEL) if (EDGE - MARGIN + tap) % 8 == residue
        ]
        shifted = padded[residue : residue + length + 24, :]
        for tap in offsets:
            start = EDGE - MARGIN + tap - residue
            weight = KERNEL - 1 - tap if reverse else tap
            total = total + taps[weight : weight + 1, :] * shifted[start : start + length, :]
    return total


COLUMNS = 128


def conv_up(low, frames, high, kernel, routes, send, experts, n_y):
    length, width = frames.shape
    slots = experts * CAP

    def body(low_ref, frames_ref, high_ref, kernel_ref, routes_ref, _, mix_ref, hid_ref, out_ref, pad):
        pad[:EDGE] = low_ref[...].astype(F32)
        pad[EDGE : EDGE + length] = frames_ref[...].astype(F32)
        pad[EDGE + length :] = high_ref[...].astype(F32)

        def step(index, carry):
            columns = pl.ds(pl.multiple_of(index * COLUMNS, COLUMNS), COLUMNS)
            mixing = tap_sum(pad, kernel_ref, columns, length, False)
            mix_ref[:, columns] = mixing
            own = pad[EDGE : EDGE + length, columns]
            hid_ref[:, columns] = (own + mixing * jax.nn.sigmoid(mixing)).astype(BF16)
            return carry

        lax.fori_loop(0, width // COLUMNS, step, 0)
        first, second = slot_masks(routes_ref, experts, n_y)
        out_ref[...] = dot(first + second, hid_ref[...], (0, 0)).astype(BF16)

    operands = (low, frames, high, kernel, routes)
    return pl.pallas_call(
        body,
        grid=(1,),
        in_specs=[pl.BlockSpec(o.shape, lambda i: (0, 0)) for o in operands]
        + [pl.BlockSpec(memory_space=pl.ANY)],
        out_specs=(
            pl.BlockSpec((length, width), lambda i: (0, 0)),
            pl.BlockSpec((length, width), lambda i: (0, 0)),
            pl.BlockSpec((slots, width), lambda i: (0, 0)),
        ),
        out_shape=(
            shape_of((length, width), F32),
            shape_of((length, width), BF16),
            shape_of((slots, 2 * width), BF16),
        ),
        input_output_aliases={5: 2},
        scratch_shapes=[pltpu.VMEM((length + 2 * EDGE, width), F32)],
        compiler_params=params(32),
        cost_estimate=COST,
        name="conv_up",
    )(*operands, send)


TILE = 512


def copy_all(copies):
    for copy in copies:
        copy.start()
    for copy in copies:
        copy.wait()


def pack_weights(spots, w_in, w_out):
    _, width, hidden = w_in.shape
    pieces = width // hidden
    half = width // 2

    def body(spots_ref, in_ref, out_ref, own_ref, first_up, first_down, next_up, next_down, sems):
        copies = []

        def move(source, target):
            copies.append(pltpu.make_async_copy(source, target, sems.at[len(copies)]))

        def pack(steps, low, high, ref, offset):
            spot = spots_ref[steps]
            move(
                in_ref.at[spot, pl.ds(low, high - low)],
                ref.at[pl.ds(offset, high - low), :hidden],
            )
            for start in range(low, high, hidden):
                move(
                    out_ref.at[spot, :, pl.ds(start, hidden)],
                    ref.at[pl.ds(offset + start - low, hidden), hidden:],
                )

        pack(2, 0, half, first_up, 0)
        pack(2, half, width, first_down, 0)
        pack(1, 0, width, next_up, half)
        pack(3, 0, width, next_down, half)
        pack(0, 0, width, own_ref, 0)
        copy_all(copies)

    rows = (width, half, half, width + half, width + half)
    return pl.pallas_call(
        body,
        in_specs=[pl.BlockSpec(memory_space=pltpu.SMEM)] + [pl.BlockSpec(memory_space=pl.ANY)] * 2,
        out_specs=[pl.BlockSpec(memory_space=pl.ANY)] * len(rows),
        out_shape=[shape_of((count, 2 * hidden), BF16) for count in rows],
        scratch_shapes=[pltpu.SemaphoreType.DMA((4 * (1 + pieces) + 1,))],
        compiler_params=params(16),
        cost_estimate=COST,
        name="pack_weights",
    )(spots, w_in, w_out)


def fill_first(parts, wholes):
    count = parts[0].shape[0]

    def body(*refs):
        sems = refs[-1]
        copy_all(
            [
                pltpu.make_async_copy(refs[i], refs[4 + i].at[:count], sems.at[i])
                for i in range(2)
            ]
        )

    return pl.pallas_call(
        body,
        in_specs=[pl.BlockSpec(memory_space=pl.ANY)] * 4,
        out_specs=[pl.BlockSpec(memory_space=pl.ANY)] * 2,
        out_shape=[shape_of(whole.shape, BF16) for whole in wholes],
        input_output_aliases={2: 0, 3: 1},
        scratch_shapes=[pltpu.SemaphoreType.DMA((2,))],
        compiler_params=params(16),
        cost_estimate=COST,
        name="fill_first",
    )(*parts, *wholes)


def listed_refs(quarters, refs, arrays):
    return [(refs[[id(a) for a in arrays].index(id(array))], offset) for array, offset in quarters]


def distinct(quarters):
    arrays = []
    for array, _ in quarters:
        if all(array is not other for other in arrays):
            arrays.append(array)
    return arrays


def in_block(quarters, hidden):
    return jnp.concatenate([ref[at : at + hidden, :hidden] for ref, at in quarters])


def out_block(quarters, hidden):
    return jnp.concatenate([ref[at : at + hidden, hidden:] for ref, at in quarters], axis=1)


def out_piece(quarters, piece, hidden):
    ref, offset = quarters[piece // hidden]
    return ref[offset : offset + hidden, hidden:]


def activate(refs, quarters, act_ref, pre_ref):
    hidden = act_ref.shape[1]
    width = refs[0].shape[1] // 2
    start = 0
    for ref in refs:
        held = slice(start, start + ref.shape[0])
        start += ref.shape[0]
        pre = dot(ref[:, :width], in_block(quarters, hidden), (1, 0))
        logistic = jax.nn.sigmoid(pre)
        act_ref[held, :] = (pre * logistic).astype(BF16)
        back = dot(ref[:, width:], out_block(quarters, hidden), (1, 1))
        slope = logistic * (1.0 + pre * (1.0 - logistic))
        pre_ref[held, :] = (back * slope).astype(BF16)


def weigh(refs, act_ref, pre_ref, grad_refs):
    hidden = act_ref.shape[1]
    width = refs[0].shape[1] // 2
    share = width // len(grad_refs)
    for piece in range(0, width, hidden):
        grad_ref = grad_refs[piece // share]
        inner = slice(piece % share, piece % share + hidden)
        shifted = slice(width + piece, width + piece + hidden)
        rows = jnp.concatenate([ref[:, shifted] for ref in refs])
        grad_ref[inner, hidden:] = dot(act_ref[...], rows, (0, 0)).astype(grad_ref.dtype)
        rows = jnp.concatenate([ref[:, piece : piece + hidden] for ref in refs])
        grad_ref[inner, :hidden] = dot(rows, pre_ref[...], (0, 0)).astype(grad_ref.dtype)


def block_step(rows, quarters, grad_type, shares):
    total, width = sum(part.shape[0] for part in rows), rows[0].shape[1] // 2
    hidden = quarters[0][0].shape[1] // 2
    result = [shape_of((total, hidden), BF16), shape_of((total, hidden), BF16)]
    result += [shape_of((width // shares, 2 * hidden), grad_type)] * shares
    arrays = distinct(quarters)

    def body(*refs):
        row_refs, refs = refs[: len(rows)], refs[len(rows) :]
        held = listed_refs(quarters, refs[: len(arrays)], arrays)
        act_ref, pre_ref, *grads = refs[len(arrays) :]
        activate(row_refs, held, act_ref, pre_ref)
        weigh(row_refs, act_ref, pre_ref, grads)

    return pl.pallas_call(
        body,
        out_shape=result,
        compiler_params=params(48),
        cost_estimate=COST,
        name="block_step",
    )(*rows, *arrays)


def back_to_width(half, acts, pres, packed, arrived):
    hidden = acts[0].shape[1]
    rows = acts[0].shape[0] // 2
    count = len(acts)
    width = hidden * count
    arrays = distinct([pair for quarters in packed for pair in quarters])

    def body(*refs):
        act_refs, pre_refs = refs[:count], refs[count : 2 * count]
        base = 2 * count + len(arrays)
        w_refs = [listed_refs(quarters, refs[2 * count : base], arrays) for quarters in packed]
        came, out_ref = refs[base:-1], refs[-1]
        held = slice(half * rows, (half + 1) * rows)

        def emit(columns, total):
            for ref in came:
                total = total + ref[:, columns].astype(F32)
            out_ref[:, columns] = total.astype(BF16)

        acted = jnp.concatenate([ref[held, :] for ref in act_refs], axis=1)
        graded = jnp.concatenate([ref[held, :] for ref in pre_refs], axis=1)
        for piece in range(0, width, hidden):
            spot = piece // hidden
            weight = jnp.concatenate([out_piece(quarters, piece, hidden) for quarters in w_refs])
            emit(slice(piece, piece + hidden), dot(acted, weight, (1, 0)))
            weight = jnp.concatenate(
                [q[spot][0][q[spot][1] : q[spot][1] + hidden, :hidden] for q in w_refs], axis=1
            )
            emit(slice(width + piece, width + piece + hidden), dot(graded, weight, (1, 1)))

    return pl.pallas_call(
        body,
        out_shape=shape_of((rows, 2 * width), BF16),
        compiler_params=params(48),
        cost_estimate=COST,
        name="back_to_width",
    )(*acts, *pres, *arrays, *arrived)


def mix_out(routes, gates, hidden, returned, experts, n_y):
    def body(routes_ref, gates_ref, hid_ref, out_ref, mixed_ref):
        masks = slot_masks(routes_ref, experts, n_y)
        gate = gates_ref[...]
        total = hid_ref[...].astype(F32)
        for choice in range(2):
            total = total + gate[:, choice : choice + 1] * dot(masks[choice], out_ref[...], (1, 0))
        mixed_ref[...] = total.astype(BF16)

    return pl.pallas_call(
        body,
        grid=(1,),
        in_specs=[
            pl.BlockSpec(routes.shape, lambda i: (0, 0)),
            pl.BlockSpec(gates.shape, lambda i: (0, 0)),
            pl.BlockSpec(hidden.shape, lambda i: (0, 0)),
            pl.BlockSpec((returned.shape[0], hidden.shape[1]), lambda i: (0, 0)),
        ],
        out_specs=pl.BlockSpec(hidden.shape, lambda i: (0, 0)),
        out_shape=shape_of(hidden.shape, BF16),
        compiler_params=params(32),
        cost_estimate=COST,
        name="mix_out",
    )(routes, gates, hidden, returned)


def grad_rows(routes, cotangent, mixing, returned, experts, n_y):
    def body(routes_ref, cot_ref, mix_ref, grad_ref, hidden_ref, back_ref):
        first, second = slot_masks(routes_ref, experts, n_y)
        grad = cot_ref[...].astype(F32) + dot(first + second, grad_ref[...], (1, 0))
        hidden_ref[...] = grad
        back_ref[...] = (grad * silu_slope(mix_ref[...])).astype(BF16)

    return pl.pallas_call(
        body,
        grid=(1,),
        in_specs=[
            pl.BlockSpec(routes.shape, lambda i: (0, 0)),
            pl.BlockSpec(cotangent.shape, lambda i: (0, 0)),
            pl.BlockSpec(mixing.shape, lambda i: (0, 0)),
            pl.BlockSpec((returned.shape[0], mixing.shape[1]), lambda i: (0, 1)),
        ],
        out_specs=(
            pl.BlockSpec(cotangent.shape, lambda i: (0, 0)),
            pl.BlockSpec(cotangent.shape, lambda i: (0, 0)),
        ),
        out_shape=(shape_of(cotangent.shape, F32), shape_of(cotangent.shape, BF16)),
        compiler_params=params(32),
        cost_estimate=COST,
        name="grad_rows",
    )(routes, cotangent, mixing, returned)


def conv_down(low, back, high, kernel, hidden_grad):
    length, width = back.shape

    def body(low_ref, back_ref, high_ref, kernel_ref, grad_ref, out_ref, pad):
        pad[:EDGE] = low_ref[...].astype(F32)
        pad[EDGE : EDGE + length] = back_ref[...].astype(F32)
        pad[EDGE + length :] = high_ref[...].astype(F32)

        def step(index, carry):
            columns = pl.ds(pl.multiple_of(index * COLUMNS, COLUMNS), COLUMNS)
            spread = tap_sum(pad, kernel_ref, columns, length, True)
            out_ref[:, columns] = (grad_ref[:, columns] + spread).astype(BF16)
            return carry

        lax.fori_loop(0, width // COLUMNS, step, 0)

    return pl.pallas_call(
        body,
        out_shape=shape_of((length, width), BF16),
        scratch_shapes=[pltpu.VMEM((length + 2 * EDGE, width), F32)],
        compiler_params=params(32),
        cost_estimate=COST,
        name="conv_down",
    )(low, back, high, kernel, hidden_grad)


def place_grads(spot, parts, count, held):
    hidden = parts[0].shape[1] // 2
    width = parts[0].shape[0] * len(parts)
    share = parts[0].shape[0]

    def body(spot_ref, *refs):
        part_refs = refs[: len(parts)]
        in_ref, out_ref = refs[-2:]
        for index, ref in enumerate(part_refs):
            in_ref[0, index * share : (index + 1) * share] = ref[:, :hidden].astype(F32)
            for piece in range(0, share, hidden):
                target = slice(index * share + piece, index * share + piece + hidden)
                out_ref[0, :, target] = ref[piece : piece + hidden, hidden:].astype(F32)

    return pl.pallas_call(
        body,
        grid_spec=pltpu.PrefetchScalarGridSpec(
            num_scalar_prefetch=1,
            grid=(1,),
            in_specs=[pl.BlockSpec(part.shape, lambda i, spot: (0, 0)) for part in parts]
            + [pl.BlockSpec(memory_space=pl.ANY)] * len(held),
            out_specs=(
                pl.BlockSpec((1, width, hidden), lambda i, spot: (spot[0], 0, 0)),
                pl.BlockSpec((1, hidden, width), lambda i, spot: (spot[0], 0, 0)),
            ),
        ),
        out_shape=(
            shape_of((count, width, hidden), F32),
            shape_of((count, hidden, width), F32),
        ),
        input_output_aliases={1 + len(parts) + index: index for index in range(len(held))},
        compiler_params=params(32),
        cost_estimate=COST,
        name="place_grads",
    )(spot, *parts, *held)


def edges(block):
    count = lax.axis_size("y") * lax.axis_size("core")
    forward = [(i, i + 1) for i in range(count - 1)]
    backward = [(target, source) for source, target in forward]
    low = lax.ppermute(block[-EDGE:], ("y", "core"), forward)
    high = lax.ppermute(block[:EDGE], ("y", "core"), backward)
    return low, high


def turn(block, steps):
    count = lax.axis_size("y")
    return lax.ppermute(block, "y", [(i, (i + steps) % count) for i in range(count)])


def swap(block):
    return lax.ppermute(block, "core", [(0, 1), (1, 0)])


def exchange(rows, groups):
    grouped = rows.reshape(groups, CAP, rows.shape[1])
    moved = lax.all_to_all(grouped, ("y", "exp"), split_axis=0, concat_axis=0, tiled=True)
    return moved.reshape(rows.shape)


def per_device(frames, conv_kernel, routes, gates, w_in, w_out, cotangent):
    n_y = lax.axis_size("y")
    n_exp = lax.axis_size("exp")
    groups = n_y * n_exp
    experts = w_in.shape[0] * n_exp
    y = lax.axis_index("y")
    frames, routes, gates, cotangent = frames[0], routes[0], gates[0], cotangent[0]
    spots = (y + jnp.arange(n_y, dtype=jnp.int32)) % n_y

    low, high = edges(frames)
    own_block, first_up, first_down, next_up, next_down = pack_weights(spots, w_in, w_out)
    first_up, first_down = turn(first_up, 1), turn(first_down, -1)

    send = down_slots(routes, gates, cotangent, experts, n_y)
    mixing, hidden, send = conv_up(low, frames, high, conv_kernel, routes, send, experts, n_y)
    send, first_up, first_down = lax.optimization_barrier((send, first_up, first_down))
    own = exchange(send, groups)
    next_up, next_down = fill_first((first_up, first_down), (next_up, next_down))
    next_up, next_down = turn(next_up, 1), turn(next_down, -1)
    middle = own.shape[0] // 2
    rows = [own, swap(own[:middle]), swap(own[middle:])]

    step = w_in.shape[2]

    def quarters(array, begin, count):
        return [(array, begin + index * step) for index in range(count)]

    acts, pres, grads, packed = {}, {}, {}, {0: quarters(own_block, 0, 4)}
    acts[0], pres[0], *grads[0] = block_step(rows, packed[0], F32, 1)
    acts[0], next_up, next_down = lax.optimization_barrier((acts[0], next_up, next_down))
    packed[2] = quarters(next_up, 0, 2) + quarters(next_down, 0, 2)
    packed[1] = quarters(next_up, 2 * step, 4)
    packed[3] = quarters(next_down, 2 * step, 4)
    acts[2], pres[2], up, down = block_step(rows, packed[2], BF16, 2)
    up, down = turn(up, 1), turn(down, -1)
    for steps in (1, 3):
        acts[steps], pres[steps], *grads[steps] = block_step(rows, packed[steps], BF16, 2)
        grads[steps] = [turn(part, -steps) for part in grads[steps]]
    acts[3], up, down = lax.optimization_barrier((acts[3], up, down))
    grads[2] = [turn(up, 1), turn(down, -1)]
    listed = [[held[steps] for steps in packed] for held in (acts, pres, packed)]
    arrived = swap(back_to_width(1, *listed, []))
    result = back_to_width(0, *listed, [arrived])
    result, grads[1][0], grads[3][0] = lax.optimization_barrier((result, grads[1][0], grads[3][0]))
    returned = exchange(result, groups)

    held = ()
    for steps in (0,):
        held = place_grads(spots[steps : steps + 1], grads[steps], n_y, held)
    returned, *held = lax.optimization_barrier((returned, *held))
    hidden_grad, back = grad_rows(routes, cotangent, mixing, returned, experts, n_y)
    low, high = edges(back)
    frames_grad = conv_down(low, back, high, conv_kernel, hidden_grad)
    mixed = mix_out(routes, gates, hidden, returned, experts, n_y)
    for steps in (1, 3, 2):
        held = place_grads(spots[steps : steps + 1], grads[steps], n_y, held)
    w_in_grad, w_out_grad = held
    return (mixed[None], frames_grad[None], w_in_grad, w_out_grad)


def solution(mesh):
    cores = 2
    n_seq, n_exp = mesh.devices.shape
    split = Mesh(mesh.devices.reshape(n_seq // cores, cores, n_exp), ("y", "core", "exp"))
    seq = ("y", "core")
    in_specs = (
        P("exp", seq, None),
        P(),
        P("exp", seq, None),
        P("exp", seq, None),
        P("exp", None, seq),
        P("exp", seq, None),
        P("exp", seq, None),
    )
    out_specs = (
        P("exp", seq, None),
        P("exp", seq, None),
        P("exp", None, seq),
        P("exp", seq, None),
    )
    return jax.shard_map(
        per_device, mesh=split, in_specs=in_specs, out_specs=out_specs, check_vma=False
    )
```

```python
import jax
import jax.numpy as jnp
from jax import lax
from jax.experimental import pallas as pl
from jax.experimental.pallas import tpu as pltpu
from jax.sharding import Mesh, PartitionSpec as P

KERNEL = 31
MARGIN = (KERNEL - 1) // 2
CAP = 8
EDGE = 16
BF16 = jnp.bfloat16
F32 = jnp.float32


def shape_of(dims, dtype):
    return jax.ShapeDtypeStruct(dims, dtype)


def params(mib):
    return pltpu.CompilerParams(vmem_limit_bytes=mib << 20)


COST = pl.CostEstimate(flops=1, bytes_accessed=1, transcendentals=0)


def silu_slope(values):
    logistic = jax.nn.sigmoid(values)
    return logistic * (1.0 + values * (1.0 - logistic))


def dot(left, right, dims):
    return lax.dot_general(left, right, ((dims[:1], dims[1:]), ((), ())), preferred_element_type=F32)


def slot_masks(routes_ref, experts, n_y):
    length = routes_ref.shape[0]
    n_exp = experts // n_y
    slots = experts * CAP
    routes = routes_ref[...]
    lane = lax.broadcasted_iota(jnp.int32, (length, experts), 1)
    before = (
        lax.broadcasted_iota(jnp.int32, (length, length), 1)
        < lax.broadcasted_iota(jnp.int32, (length, length), 0)
    ).astype(F32).astype(BF16)
    place = lax.broadcasted_iota(jnp.int32, (length, slots), 1)
    base = jnp.zeros((1, experts), F32)
    masks = []
    for choice in range(2):
        expert = routes[:, choice : choice + 1]
        named = (lane == expert).astype(F32)
        earlier = dot(before, named.astype(BF16), (1, 0)) + base
        rank = jnp.sum(named * earlier, axis=1, keepdims=True).astype(jnp.int32)
        base = base + jnp.sum(named, axis=0, keepdims=True)
        start = (expert % n_y) * n_exp + expert // n_y
        masks.append((place == start * CAP + rank).astype(F32).astype(BF16))
    return masks


def down_slots(routes, gates, cotangent, experts, n_y):
    length, width = cotangent.shape

    def body(routes_ref, gates_ref, cot_ref, out_ref):
        masks = slot_masks(routes_ref, experts, n_y)
        cot = cot_ref[...].astype(F32)
        gate = gates_ref[...]
        total = None
        for choice in range(2):
            rows = (gate[:, choice : choice + 1] * cot).astype(BF16)
            part = dot(masks[choice], rows, (0, 0))
            total = part if total is None else total + part
        out_ref[...] = total.astype(BF16)

    return pl.pallas_call(
        body,
        grid=(1,),
        in_specs=[
            pl.BlockSpec(routes.shape, lambda i: (0, 0)),
            pl.BlockSpec(gates.shape, lambda i: (0, 0)),
            pl.BlockSpec(cotangent.shape, lambda i: (0, 0)),
        ],
        out_specs=pl.BlockSpec((experts * CAP, width), lambda i: (0, 1)),
        out_shape=shape_of((experts * CAP, 2 * width), BF16),
        compiler_params=params(32),
        cost_estimate=COST,
        name="down_slots",
    )(routes, gates, cotangent)


def tap_sum(pad_ref, kernel_ref, columns, length, reverse):
    padded = pad_ref[:, columns]
    taps = kernel_ref[:, columns]
    total = jnp.zeros((length, padded.shape[1]), F32)
    for residue in range(8):
        offsets = [
            tap for tap in range(KERNEL) if (EDGE - MARGIN + tap) % 8 == residue
        ]
        shifted = padded[residue : residue + length + 24, :]
        for tap in offsets:
            start = EDGE - MARGIN + tap - residue
            weight = KERNEL - 1 - tap if reverse else tap
            total = total + taps[weight : weight + 1, :] * shifted[start : start + length, :]
    return total


COLUMNS = 128


def conv_up(low, frames, high, kernel, routes, send, experts, n_y):
    length, width = frames.shape
    slots = experts * CAP

    def body(low_ref, frames_ref, high_ref, kernel_ref, routes_ref, _, mix_ref, hid_ref, out_ref, pad):
        pad[:EDGE] = low_ref[...].astype(F32)
        pad[EDGE : EDGE + length] = frames_ref[...].astype(F32)
        pad[EDGE + length :] = high_ref[...].astype(F32)

        def step(index, carry):
            columns = pl.ds(pl.multiple_of(index * COLUMNS, COLUMNS), COLUMNS)
            mixing = tap_sum(pad, kernel_ref, columns, length, False)
            mix_ref[:, columns] = mixing
            own = pad[EDGE : EDGE + length, columns]
            hid_ref[:, columns] = (own + mixing * jax.nn.sigmoid(mixing)).astype(BF16)
            return carry

        lax.fori_loop(0, width // COLUMNS, step, 0)
        first, second = slot_masks(routes_ref, experts, n_y)
        out_ref[...] = dot(first + second, hid_ref[...], (0, 0)).astype(BF16)

    operands = (low, frames, high, kernel, routes)
    return pl.pallas_call(
        body,
        grid=(1,),
        in_specs=[pl.BlockSpec(o.shape, lambda i: (0, 0)) for o in operands]
        + [pl.BlockSpec(memory_space=pl.ANY)],
        out_specs=(
            pl.BlockSpec((length, width), lambda i: (0, 0)),
            pl.BlockSpec((length, width), lambda i: (0, 0)),
            pl.BlockSpec((slots, width), lambda i: (0, 0)),
        ),
        out_shape=(
            shape_of((length, width), F32),
            shape_of((length, width), BF16),
            shape_of((slots, 2 * width), BF16),
        ),
        input_output_aliases={5: 2},
        scratch_shapes=[pltpu.VMEM((length + 2 * EDGE, width), F32)],
        compiler_params=params(32),
        cost_estimate=COST,
        name="conv_up",
    )(*operands, send)


TILE = 512


def copy_all(copies):
    for copy in copies:
        copy.start()
    for copy in copies:
        copy.wait()


def pack_weights(spots, w_in, w_out):
    _, width, hidden = w_in.shape
    pieces = width // hidden
    half = width // 2
    rows = (width, half, half, width, width)

    def body(spots_ref, in_ref, out_ref, own_ref, far_up, far_down, near_up, near_down, sems):
        copies = []

        def move(source, target):
            copies.append(pltpu.make_async_copy(source, target, sems.at[len(copies)]))

        def pack(steps, low, high, ref):
            spot = spots_ref[steps]
            move(in_ref.at[spot, pl.ds(low, high - low)], ref.at[:, :hidden])
            for start in range(low, high, hidden):
                move(
                    out_ref.at[spot, :, pl.ds(start, hidden)],
                    ref.at[pl.ds(start - low, hidden), hidden:],
                )

        pack(2, 0, half, far_up)
        pack(2, half, width, far_down)
        pack(1, 0, width, near_up)
        pack(3, 0, width, near_down)
        pack(0, 0, width, own_ref)
        copy_all(copies)

    return pl.pallas_call(
        body,
        in_specs=[pl.BlockSpec(memory_space=pltpu.SMEM)] + [pl.BlockSpec(memory_space=pl.ANY)] * 2,
        out_specs=[pl.BlockSpec(memory_space=pl.ANY)] * len(rows),
        out_shape=[shape_of((count, 2 * hidden), BF16) for count in rows],
        scratch_shapes=[pltpu.SemaphoreType.DMA((4 * pieces + 5,))],
        compiler_params=params(16),
        cost_estimate=COST,
        name="pack_weights",
    )(spots, w_in, w_out)


def listed_refs(quarters, refs, arrays):
    return [(refs[[id(a) for a in arrays].index(id(array))], offset) for array, offset in quarters]


def distinct(quarters):
    arrays = []
    for array, _ in quarters:
        if all(array is not other for other in arrays):
            arrays.append(array)
    return arrays


def in_block(quarters, hidden):
    return jnp.concatenate([ref[at : at + hidden, :hidden] for ref, at in quarters])


def out_block(quarters, hidden):
    return jnp.concatenate([ref[at : at + hidden, hidden:] for ref, at in quarters], axis=1)


def out_piece(quarters, piece, hidden):
    ref, offset = quarters[piece // hidden]
    return ref[offset : offset + hidden, hidden:]


def activate(refs, quarters, act_ref, pre_ref):
    hidden = act_ref.shape[1]
    width = refs[0].shape[1] // 2
    start = 0
    for ref in refs:
        held = slice(start, start + ref.shape[0])
        start += ref.shape[0]
        pre = dot(ref[:, :width], in_block(quarters, hidden), (1, 0))
        logistic = jax.nn.sigmoid(pre)
        act_ref[held, :] = (pre * logistic).astype(BF16)
        back = dot(ref[:, width:], out_block(quarters, hidden), (1, 1))
        slope = logistic * (1.0 + pre * (1.0 - logistic))
        pre_ref[held, :] = (back * slope).astype(BF16)


def weigh(refs, act_ref, pre_ref, grad_refs):
    hidden = act_ref.shape[1]
    width = refs[0].shape[1] // 2
    share = width // len(grad_refs)
    for piece in range(0, width, hidden):
        grad_ref = grad_refs[piece // share]
        inner = slice(piece % share, piece % share + hidden)
        shifted = slice(width + piece, width + piece + hidden)
        rows = jnp.concatenate([ref[:, shifted] for ref in refs])
        grad_ref[inner, hidden:] = dot(act_ref[...], rows, (0, 0)).astype(grad_ref.dtype)
        rows = jnp.concatenate([ref[:, piece : piece + hidden] for ref in refs])
        grad_ref[inner, :hidden] = dot(rows, pre_ref[...], (0, 0)).astype(grad_ref.dtype)


def block_step(rows, quarters, grad_type, shares):
    total, width = sum(part.shape[0] for part in rows), rows[0].shape[1] // 2
    hidden = quarters[0][0].shape[1] // 2
    result = [shape_of((total, hidden), BF16), shape_of((total, hidden), BF16)]
    result += [shape_of((width // shares, 2 * hidden), grad_type)] * shares
    arrays = distinct(quarters)

    def body(*refs):
        row_refs, refs = refs[: len(rows)], refs[len(rows) :]
        held = listed_refs(quarters, refs[: len(arrays)], arrays)
        act_ref, pre_ref, *grads = refs[len(arrays) :]
        activate(row_refs, held, act_ref, pre_ref)
        weigh(row_refs, act_ref, pre_ref, grads)

    return pl.pallas_call(
        body,
        out_shape=result,
        compiler_params=params(48),
        cost_estimate=COST,
        name="block_step",
    )(*rows, *arrays)


def back_to_width(half, acts, pres, packed, arrived):
    hidden = acts[0].shape[1]
    rows = acts[0].shape[0] // 2
    count = len(acts)
    width = hidden * count
    arrays = distinct([pair for quarters in packed for pair in quarters])

    def body(*refs):
        act_refs, pre_refs = refs[:count], refs[count : 2 * count]
        base = 2 * count + len(arrays)
        w_refs = [listed_refs(quarters, refs[2 * count : base], arrays) for quarters in packed]
        came, out_ref = refs[base:-1], refs[-1]
        held = slice(half * rows, (half + 1) * rows)

        def emit(columns, total):
            for ref in came:
                total = total + ref[:, columns].astype(F32)
            out_ref[:, columns] = total.astype(BF16)

        acted = jnp.concatenate([ref[held, :] for ref in act_refs], axis=1)
        graded = jnp.concatenate([ref[held, :] for ref in pre_refs], axis=1)
        for piece in range(0, width, hidden):
            spot = piece // hidden
            weight = jnp.concatenate([out_piece(quarters, piece, hidden) for quarters in w_refs])
            emit(slice(piece, piece + hidden), dot(acted, weight, (1, 0)))
            weight = jnp.concatenate(
                [q[spot][0][q[spot][1] : q[spot][1] + hidden, :hidden] for q in w_refs], axis=1
            )
            emit(slice(width + piece, width + piece + hidden), dot(graded, weight, (1, 1)))

    return pl.pallas_call(
        body,
        out_shape=shape_of((rows, 2 * width), BF16),
        compiler_params=params(48),
        cost_estimate=COST,
        name="back_to_width",
    )(*acts, *pres, *arrays, *arrived)


def mix_out(routes, gates, hidden, returned, experts, n_y):
    def body(routes_ref, gates_ref, hid_ref, out_ref, mixed_ref):
        masks = slot_masks(routes_ref, experts, n_y)
        gate = gates_ref[...]
        total = hid_ref[...].astype(F32)
        for choice in range(2):
            total = total + gate[:, choice : choice + 1] * dot(masks[choice], out_ref[...], (1, 0))
        mixed_ref[...] = total.astype(BF16)

    return pl.pallas_call(
        body,
        grid=(1,),
        in_specs=[
            pl.BlockSpec(routes.shape, lambda i: (0, 0)),
            pl.BlockSpec(gates.shape, lambda i: (0, 0)),
            pl.BlockSpec(hidden.shape, lambda i: (0, 0)),
            pl.BlockSpec((returned.shape[0], hidden.shape[1]), lambda i: (0, 0)),
        ],
        out_specs=pl.BlockSpec(hidden.shape, lambda i: (0, 0)),
        out_shape=shape_of(hidden.shape, BF16),
        compiler_params=params(32),
        cost_estimate=COST,
        name="mix_out",
    )(routes, gates, hidden, returned)


def grad_rows(routes, cotangent, mixing, returned, experts, n_y):
    def body(routes_ref, cot_ref, mix_ref, grad_ref, hidden_ref, back_ref):
        first, second = slot_masks(routes_ref, experts, n_y)
        grad = cot_ref[...].astype(F32) + dot(first + second, grad_ref[...], (1, 0))
        hidden_ref[...] = grad
        back_ref[...] = (grad * silu_slope(mix_ref[...])).astype(BF16)

    return pl.pallas_call(
        body,
        grid=(1,),
        in_specs=[
            pl.BlockSpec(routes.shape, lambda i: (0, 0)),
            pl.BlockSpec(cotangent.shape, lambda i: (0, 0)),
            pl.BlockSpec(mixing.shape, lambda i: (0, 0)),
            pl.BlockSpec((returned.shape[0], mixing.shape[1]), lambda i: (0, 1)),
        ],
        out_specs=(
            pl.BlockSpec(cotangent.shape, lambda i: (0, 0)),
            pl.BlockSpec(cotangent.shape, lambda i: (0, 0)),
        ),
        out_shape=(shape_of(cotangent.shape, F32), shape_of(cotangent.shape, BF16)),
        compiler_params=params(32),
        cost_estimate=COST,
        name="grad_rows",
    )(routes, cotangent, mixing, returned)


def conv_down(low, back, high, kernel, hidden_grad):
    length, width = back.shape

    def body(low_ref, back_ref, high_ref, kernel_ref, grad_ref, out_ref, pad):
        pad[:EDGE] = low_ref[...].astype(F32)
        pad[EDGE : EDGE + length] = back_ref[...].astype(F32)
        pad[EDGE + length :] = high_ref[...].astype(F32)

        def step(index, carry):
            columns = pl.ds(pl.multiple_of(index * COLUMNS, COLUMNS), COLUMNS)
            spread = tap_sum(pad, kernel_ref, columns, length, True)
            out_ref[:, columns] = (grad_ref[:, columns] + spread).astype(BF16)
            return carry

        lax.fori_loop(0, width // COLUMNS, step, 0)

    return pl.pallas_call(
        body,
        out_shape=shape_of((length, width), BF16),
        scratch_shapes=[pltpu.VMEM((length + 2 * EDGE, width), F32)],
        compiler_params=params(32),
        cost_estimate=COST,
        name="conv_down",
    )(low, back, high, kernel, hidden_grad)


def place_grads(spot, parts, count, held):
    hidden = parts[0].shape[1] // 2
    width = parts[0].shape[0] * len(parts)
    share = parts[0].shape[0]

    def body(spot_ref, *refs):
        part_refs = refs[: len(parts)]
        in_ref, out_ref = refs[-2:]
        for index, ref in enumerate(part_refs):
            in_ref[0, index * share : (index + 1) * share] = ref[:, :hidden].astype(F32)
            for piece in range(0, share, hidden):
                target = slice(index * share + piece, index * share + piece + hidden)
                out_ref[0, :, target] = ref[piece : piece + hidden, hidden:].astype(F32)

    return pl.pallas_call(
        body,
        grid_spec=pltpu.PrefetchScalarGridSpec(
            num_scalar_prefetch=1,
            grid=(1,),
            in_specs=[pl.BlockSpec(part.shape, lambda i, spot: (0, 0)) for part in parts]
            + [pl.BlockSpec(memory_space=pl.ANY)] * len(held),
            out_specs=(
                pl.BlockSpec((1, width, hidden), lambda i, spot: (spot[0], 0, 0)),
                pl.BlockSpec((1, hidden, width), lambda i, spot: (spot[0], 0, 0)),
            ),
        ),
        out_shape=(
            shape_of((count, width, hidden), F32),
            shape_of((count, hidden, width), F32),
        ),
        input_output_aliases={1 + len(parts) + index: index for index in range(len(held))},
        compiler_params=params(32),
        cost_estimate=COST,
        name="place_grads",
    )(spot, *parts, *held)


def picked(index, values):
    result = values[-1]
    for spot, value in enumerate(values[:-1]):
        result = jnp.where(index == spot, value, result)
    return result


def place_halves(spots, chosen, parts, count, held):
    hidden = parts[0][0].shape[1] // 2
    half = 2 * hidden
    amount = len(parts)
    steps, sides = zip(*chosen)

    def body(spots_ref, *refs):
        in_ref, out_ref = refs[-2:]
        for index in range(amount):

            @pl.when(pl.program_id(0) == index)
            def _():
                in_ref[0] = refs[index][:, :hidden].astype(F32)
                for piece in range(0, half, hidden):
                    rows = slice(piece, piece + hidden)
                    out_ref[0, :, rows] = refs[index][rows, hidden:].astype(F32)

    return pl.pallas_call(
        body,
        grid_spec=pltpu.PrefetchScalarGridSpec(
            num_scalar_prefetch=1,
            grid=(amount,),
            in_specs=[
                pl.BlockSpec((half, 2 * hidden), lambda i, spots, side=side: (side, 0))
                for _, side in parts
            ]
            + [pl.BlockSpec(memory_space=pl.ANY)] * 2,
            out_specs=(
                pl.BlockSpec((1, half, hidden), lambda i, spots: (spots[picked(i, steps)], picked(i, sides), 0)),
                pl.BlockSpec((1, hidden, half), lambda i, spots: (spots[picked(i, steps)], 0, picked(i, sides))),
            ),
        ),
        out_shape=(
            shape_of((count, 2 * half, hidden), F32),
            shape_of((count, hidden, 2 * half), F32),
        ),
        input_output_aliases={1 + amount: 0, 2 + amount: 1},
        compiler_params=params(32),
        cost_estimate=COST,
        name="place_halves",
    )(spots, *[part for part, _ in parts], *held)


def edges(block):
    count = lax.axis_size("y") * lax.axis_size("core")
    forward = [(i, i + 1) for i in range(count - 1)]
    backward = [(target, source) for source, target in forward]
    low = lax.ppermute(block[-EDGE:], ("y", "core"), forward)
    high = lax.ppermute(block[:EDGE], ("y", "core"), backward)
    return low, high


def turn(block, steps):
    count = lax.axis_size("y")
    return lax.ppermute(block, "y", [(i, (i + steps) % count) for i in range(count)])


def swap(block):
    return lax.ppermute(block, "core", [(0, 1), (1, 0)])


def exchange(rows, groups):
    grouped = rows.reshape(groups, CAP, rows.shape[1])
    moved = lax.all_to_all(grouped, ("y", "exp"), split_axis=0, concat_axis=0, tiled=True)
    return moved.reshape(rows.shape)


def per_device(frames, conv_kernel, routes, gates, w_in, w_out, cotangent):
    n_y = lax.axis_size("y")
    n_exp = lax.axis_size("exp")
    groups = n_y * n_exp
    experts = w_in.shape[0] * n_exp
    y = lax.axis_index("y")
    frames, routes, gates, cotangent = frames[0], routes[0], gates[0], cotangent[0]
    spots = (y + jnp.arange(n_y, dtype=jnp.int32)) % n_y

    low, high = edges(frames)
    own_block, far_up, far_down, near_up, near_down = pack_weights(spots, w_in, w_out)
    far_up, far_down = turn(far_up, 1), turn(far_down, -1)
    near_up, near_down = turn(near_up, 1), turn(near_down, -1)

    send = down_slots(routes, gates, cotangent, experts, n_y)
    mixing, hidden, send = conv_up(low, frames, high, conv_kernel, routes, send, experts, n_y)
    send, far_up, far_down, near_up, near_down = lax.optimization_barrier(
        (send, far_up, far_down, near_up, near_down)
    )
    own = exchange(send, groups)
    far_up, far_down = turn(far_up, 1), turn(far_down, -1)
    own, far_up, far_down = lax.optimization_barrier((own, far_up, far_down))
    middle = own.shape[0] // 2
    rows = [own, swap(own[:middle]), swap(own[middle:])]

    step = w_in.shape[2]

    def quarters(array, begin, count):
        return [(array, begin + index * step) for index in range(count)]

    acts, pres, grads, packed = {}, {}, {}, {0: quarters(own_block, 0, 4)}
    acts[0], pres[0], *grads[0] = block_step(rows, packed[0], F32, 1)
    packed[2] = quarters(far_up, 0, 2) + quarters(far_down, 0, 2)
    acts[2], pres[2], up, down = block_step(rows, packed[2], BF16, 2)
    up, down = turn(up, 1), turn(down, -1)
    acts[2], near_up, near_down = lax.optimization_barrier((acts[2], near_up, near_down))
    packed[1], packed[3] = quarters(near_up, 0, 4), quarters(near_down, 0, 4)
    for steps in (1, 3):
        acts[steps], pres[steps], *grads[steps] = block_step(rows, packed[steps], BF16, 2)
        grads[steps][0] = turn(grads[steps][0], -steps)
    acts[3], up, down = lax.optimization_barrier((acts[3], up, down))
    late_up = jnp.concatenate([grads[3][1], up])
    late_down = jnp.concatenate([grads[1][1], down])
    listed = [[held[steps] for steps in packed] for held in (acts, pres, packed)]
    arrived = swap(back_to_width(1, *listed, []))
    result = back_to_width(0, *listed, [arrived])
    result, grads[1][0], grads[3][0], late_up, late_down = lax.optimization_barrier(
        (result, grads[1][0], grads[3][0], late_up, late_down)
    )
    late_up, late_down = turn(late_up, 1), turn(late_down, -1)
    returned = exchange(result, groups)

    held = place_grads(spots, grads[0], n_y, ())

    held = place_halves(spots, ((1, 0), (3, 0)), [(grads[1][0], 0), (grads[3][0], 0)], n_y, held)
    returned, *held = lax.optimization_barrier((returned, *held))
    hidden_grad, back = grad_rows(routes, cotangent, mixing, returned, experts, n_y)
    low, high = edges(back)
    frames_grad = conv_down(low, back, high, conv_kernel, hidden_grad)
    mixed = mix_out(routes, gates, hidden, returned, experts, n_y)
    frames_grad, mixed, late_up, late_down = lax.optimization_barrier(
        (frames_grad, mixed, late_up, late_down)
    )
    w_in_grad, w_out_grad = place_halves(
        spots, ((1, 1), (3, 1), (2, 0), (2, 1)), [(late_down, 0), (late_up, 0), (late_up, 1), (late_down, 1)], n_y, held
    )
    return (mixed[None], frames_grad[None], w_in_grad, w_out_grad)


def solution(mesh):
    cores = 2
    n_seq, n_exp = mesh.devices.shape
    split = Mesh(mesh.devices.reshape(n_seq // cores, cores, n_exp), ("y", "core", "exp"))
    seq = ("y", "core")
    in_specs = (
        P("exp", seq, None),
        P(),
        P("exp", seq, None),
        P("exp", seq, None),
        P("exp", None, seq),
        P("exp", seq, None),
        P("exp", seq, None),
    )
    out_specs = (
        P("exp", seq, None),
        P("exp", seq, None),
        P("exp", None, seq),
        P("exp", seq, None),
    )
    return jax.shard_map(
        per_device, mesh=split, in_specs=in_specs, out_specs=out_specs, check_vma=False
    )
```
